512 devices in a mesh: tensor: 8 (over x, core), dp: 64 (over y, z).
Axes of the slice: x: 4, y: 8, z: 8, core: 2. Of those that a mesh axis runs over, the one named last changes fastest.
Arguments:
- inputs: bfloat16 [16384, 8192], P('dp', 'tensor'), may hold values from -6 to 6
- frozen_value_weight: bfloat16 [8192, 1024], P(None, 'tensor'), may hold values from -0.0625 to 0.0625
- adapter_down_matrix: bfloat16 [64, 8192, 16], P('dp', 'tensor'), may hold values from -0.0625 to 0.0625
- adapter_up_matrix: bfloat16 [64, 16, 1024], P('dp', None, 'tensor'), may hold values from -1.5 to 1.5
- value_cotangent: bfloat16 [16384, 1024], P('dp', 'tensor'), may hold values from -6 to 6
- tenant_of_block: int32 [128], P('dp'), may hold values from 0 to 63
- quotas: int32 [64], replicated, may hold values from 128 to 1023
Outputs:
- adapted_values: bfloat16 [16384, 1024], P('dp', 'tensor')
- gradient_inputs: bfloat16 [16384, 8192], P('dp', 'tensor')
- down_grad: float32 [64, 8192, 16], P('dp', 'tensor')
- gradient_up_matrix: float32 [64, 16, 1024], P('dp', None, 'tensor')
The draws below stay inside these ranges and needn't reach their ends.
All inputs are finite; a program needn't handle non-finite values.
Results may differ from the reference program's by a relative error of at most 0.015.
Values may be sent and summed in bfloat16 or wider, within the bound.
A program may use at most 64 MiB of HBM per device.

```python
import math
import jax
import jax.numpy as jnp
import numpy as np
from jax import lax

MODEL_WIDTH = 8192
VALUE_WIDTH = 1024
ADAPTER_RANK = 16
BLOCK = 128
ADAPTER_TOTAL = 64
TOKEN_TOTAL = 16384
NBLK = 128
N_TENSOR = 8


def place_ends(drawn, key, low, high):
    spot = [jax.random.randint(jax.random.fold_in(key, axis), (), 0, length) for axis, length in enumerate(drawn.shape)]
    longest = drawn.shape.index(max(drawn.shape))
    neighbour = spot[:longest] + [(spot[longest] + 1) % drawn.shape[longest]] + spot[longest + 1:]
    return drawn.at[tuple(spot)].set(low).at[tuple(neighbour)].set(high)


def shard_levels(key, extent, cuts, smallest, top_value):
    loudness, own = 1.0, jax.random.fold_in(key, 6)
    for axis_at, shards_of in cuts:
        heights = jnp.exp(jax.random.uniform(jax.random.fold_in(own, axis_at), (shards_of,), jnp.float32, smallest / len(cuts), top_value / len(cuts)))
        loudness = loudness * jnp.repeat(heights, extent[axis_at] // shards_of).reshape([-1 if axis == axis_at else 1 for axis in range(len(extent))])
    return loudness


def cumulative_ranks(amount, slope):
    weights = [(1 << 20) // math.isqrt(rank ** slope) + 1 for rank in range(1, amount + 1)]
    spread = 1 + sum(weights) // (1 << 30)
    return np.cumsum(np.array([max(1, weight // spread) for weight in weights]))


def ranked_ids(rng, shape, amount, slope):
    table = cumulative_ranks(amount, slope)
    pick = jax.random.randint(jax.random.fold_in(rng, 1), shape, 0, int(table[amount - 1]))
    rank = jnp.searchsorted(jnp.asarray(table, jnp.int32), pick, side="right")
    return jax.random.permutation(jax.random.fold_in(rng, 2), amount)[rank].astype(jnp.int32)


def bell_draw(stream_key, shape, spread, most, cuts=(), held_as=jnp.bfloat16):
    result = jax.random.normal(stream_key, shape, jnp.float32) * spread
    if len(cuts) > 0:
        result = shard_levels(stream_key, shape, cuts, -0.22, 0.18) * result
    return jnp.clip(result, min=-most, max=most).astype(held_as)


def setup_inputs(seed: int = 0) -> dict:
    arg_keys = jax.random.split(jax.random.key(seed), 8)
    return {
        "inputs": bell_draw(arg_keys[0], (TOKEN_TOTAL, MODEL_WIDTH), 1.0, 6.0, ((0, 64), (1, 8))),
        "frozen_value_weight": bell_draw(arg_keys[1], (MODEL_WIDTH, VALUE_WIDTH), MODEL_WIDTH ** -0.5, 0.0625, ((1, 8),)),
        "adapter_down_matrix": bell_draw(arg_keys[2], (ADAPTER_TOTAL, MODEL_WIDTH, ADAPTER_RANK), MODEL_WIDTH ** -0.5, 0.0625, ((0, 64), (1, 8))),
        "adapter_up_matrix": bell_draw(arg_keys[3], (ADAPTER_TOTAL, ADAPTER_RANK, VALUE_WIDTH), ADAPTER_RANK ** -0.5, 1.5, ((0, 64), (2, 8))),
        "value_cotangent": bell_draw(arg_keys[4], (TOKEN_TOTAL, VALUE_WIDTH), 1.0, 6.0, ((0, 64), (1, 8))),
        "tenant_of_block": place_ends(ranked_ids(arg_keys[5], (NBLK,), ADAPTER_TOTAL, 2), jax.random.fold_in(arg_keys[5], 3), 0, ADAPTER_TOTAL - 1).astype(jnp.int32),
        "quotas": place_ends(jax.random.randint(arg_keys[6], (ADAPTER_TOTAL,), BLOCK, 8 * BLOCK), jax.random.fold_in(arg_keys[6], 1), BLOCK, (8 * BLOCK) - 1).astype(jnp.int32),
    }


adapter_scale = 2.0


def reference(inputs, frozen_value_weight, adapter_down_matrix, adapter_up_matrix, value_cotangent, tenant_of_block, quotas):
    nblocks = tenant_of_block.shape[0]
    input_blocks = inputs.reshape(nblocks, BLOCK, MODEL_WIDTH)
    value_grad_blocks = value_cotangent.reshape(nblocks, BLOCK, VALUE_WIDTH)
    frozen_output = jnp.dot(inputs, frozen_value_weight, preferred_element_type=jnp.float32)

    def block_partials(packed):
        x_rows, value_grad_rows, tenant_number = packed
        down_weight = adapter_down_matrix[tenant_number]
        up_weight = adapter_up_matrix[tenant_number]
        reduced_features = jnp.dot(x_rows, down_weight, preferred_element_type=jnp.float32).astype(jnp.bfloat16)
        gradient_lowrank = (adapter_scale * lax.dot_general(value_grad_rows, up_weight, (((1,), (1,)), ((), ())), preferred_element_type=jnp.float32)).astype(jnp.bfloat16)
        raised_output = jnp.dot(reduced_features, up_weight, preferred_element_type=jnp.float32)
        adapter_input = lax.dot_general(gradient_lowrank, down_weight, (((1,), (1,)), ((), ())), preferred_element_type=jnp.float32)
        return reduced_features, gradient_lowrank, raised_output, adapter_input

    reduced_features, gradient_lowrank, raised_output, adapter_input = lax.map(block_partials, (input_blocks, value_grad_blocks, tenant_of_block))
    adapted_values = (frozen_output + adapter_scale * raised_output.reshape(TOKEN_TOTAL, VALUE_WIDTH)).astype(jnp.bfloat16)

    group = VALUE_WIDTH // N_TENSOR

    def add_group(index, running):
        dv_part = lax.dynamic_slice_in_dim(value_cotangent, index * group, group, 1)
        w_part = lax.dynamic_slice_in_dim(frozen_value_weight, index * group, group, 1)
        term = lax.dot_general(dv_part, w_part, (((1,), (1,)), ((), ())), preferred_element_type=jnp.float32)
        return running + term.astype(jnp.bfloat16).astype(jnp.float32)

    summed_gradient = lax.fori_loop(0, N_TENSOR, add_group, jnp.zeros((TOKEN_TOTAL, MODEL_WIDTH), jnp.float32))
    gradient_inputs = (summed_gradient + adapter_input.reshape(TOKEN_TOTAL, MODEL_WIDTH)).astype(jnp.bfloat16)

    onehot = (tenant_of_block[:, None] == jnp.arange(ADAPTER_TOTAL, dtype=jnp.int32)[None, :]).astype(jnp.float32)
    counts = jnp.sum(onehot, axis=0) * BLOCK
    scale = quotas.astype(jnp.float32) / jnp.maximum(counts, 1.0)
    quota_weighted = onehot * scale[None, :]
    grad_a = jnp.einsum('bnd,bnr->bdr', input_blocks.astype(jnp.float32), gradient_lowrank.astype(jnp.float32))
    up_gradient_local = jnp.einsum('bnr,bnk->brk', reduced_features.astype(jnp.float32), value_grad_blocks.astype(jnp.float32))
    down_grad = jnp.einsum('ba,bdr->adr', quota_weighted, grad_a, precision=lax.Precision.HIGHEST)
    gradient_up_matrix = adapter_scale * jnp.einsum('mw,mqf->wqf', quota_weighted, up_gradient_local, precision=lax.Precision.HIGHEST)
    return adapted_values, gradient_inputs, down_grad, gradient_up_matrix
```

```python
import functools

import jax
import jax.numpy as jnp
from jax import lax
from jax.experimental import pallas as pl
from jax.experimental.pallas import tpu as pltpu
from jax.sharding import PartitionSpec as P

MESH = pl.DeviceIdType.MESH
BLOCK = 128
LINE = 8
ADAPTER_SCALE = 2.0
BF16 = jnp.bfloat16
F32 = jnp.float32

TZ, TY, AZ, AY, SY, SZ, VAL, WGT, RANK, BASE, GZ, GY, HY, HZ, CNT = range(15)


def far_first(n):
    return sorted(range(1, n), key=lambda off: (-min(off, n - off), off))


def nt_dot(a, b):
    return lax.dot_general(a, b, (((1,), (1,)), ((), ())), preferred_element_type=F32)


def tn_dot(a, b):
    return lax.dot_general(a, b, (((0,), (0,)), ((), ())), preferred_element_type=F32)


def kernel(
    nt, ny, nz,
    ten_s, quo_s, x_hbm, w_hbm, a_hbm, b_hbm, v_hbm,
    out_ref, gin_hbm, da_ref, db_ref,
    tile, tz_v, ty_v, tz_s, ty_s, all_ten,
    xv, a1, a2, row1, col2, s1, s2, r1, r2,
    vbuf, wbuf, pbuf, bsend, ebuf, g1, g2, gz_v, gy_v, h1, h2, hz1, hz2, gin_v,
    loc, ss, rs,
):
    t = lax.axis_index("tensor")
    d = lax.axis_index("dp")
    y, z = lax.div(d, nz), lax.rem(d, nz)
    rows, feats = xv.shape
    nb = rows // BLOCK
    half = a2.shape[1]
    first = feats - half
    values = v_hbm.shape[1]
    rank = a2.shape[0]

    lines = {
        "t": (t, nt, lambda p: {"tensor": p}),
        "y": (y, ny, lambda p: {"dp": p * nz + z}),
        "z": (z, nz, lambda p: {"dp": y * nz + p}),
    }

    def remote(kind, line, src, dst, peer):
        me, _, dev = lines[line]
        return pltpu.make_async_remote_copy(
            src_ref=src, dst_ref=dst, send_sem=ss.at[kind, peer], recv_sem=rs.at[kind, me],
            device_id=dev(peer), device_id_type=MESH,
        )

    def arrived(kind, line, buf, peer):
        _, _, dev = lines[line]
        pltpu.make_async_remote_copy(
            src_ref=buf.at[peer], dst_ref=buf.at[peer], send_sem=ss.at[kind, peer],
            recv_sem=rs.at[kind, peer], device_id=dev(peer), device_id_type=MESH,
        ).wait_recv()

    def peers(line, fn):
        me, n, _ = lines[line]
        for off in far_first(n):
            fn(lax.rem(me + off, n))

    def each(line, fn):
        me, n, _ = lines[line]

        def body(off, carry):
            fn(lax.rem(me + off, n))
            return carry

        lax.fori_loop(1, n, body, 0)

    local = [
        pltpu.make_async_copy(a_hbm.at[:, pl.ds(0, first)], a1.at[:, pl.ds(0, first)], loc.at[0]),
        pltpu.make_async_copy(b_hbm, a1.at[:, pl.ds(first, values)], loc.at[1]),
        pltpu.make_async_copy(a_hbm.at[:, pl.ds(first, half)], a2, loc.at[2]),
        pltpu.make_async_copy(x_hbm, xv, loc.at[3]),
        pltpu.make_async_copy(v_hbm, vbuf.at[t], loc.at[4]),
        pltpu.make_async_copy(w_hbm.at[pl.ds(t * feats, feats)], wbuf.at[t], loc.at[5]),
    ]
    for copy in local:
        copy.start()
    lane = lax.broadcasted_iota(jnp.int32, tile.shape, 1)
    mine = jnp.full(tile.shape, -1, jnp.int32)
    for k in range(nb):
        mine = jnp.where(lane == k, ten_s[k], mine)
    tile[...] = mine
    tz_v[z] = mine
    ty_v[y] = mine

    barrier = pltpu.get_barrier_semaphore()
    for line in ("t", "y", "z"):
        dev = lines[line][2]
        each(line, lambda p: pl.semaphore_signal(barrier, inc=1, device_id=dev(p), device_id_type=MESH))
    local[0].wait()
    local[1].wait()
    local[2].wait()
    row1[z] = a1[...]
    col2[y] = a2[...]
    pl.semaphore_wait(barrier, nt + ny + nz - 3)

    peers("z", lambda p: remote(TZ, "z", tile, tz_v.at[z], p).start())
    peers("y", lambda p: remote(TY, "y", tile, ty_v.at[y], p).start())
    peers("z", lambda p: remote(AZ, "z", a1, row1.at[z], p).start())
    peers("y", lambda p: remote(AY, "y", a2, col2.at[y], p).start())
    peers("t", lambda p: remote(WGT, "t", w_hbm.at[pl.ds(p * feats, feats)], wbuf.at[t], p).start())
    local[4].wait()
    peers("t", lambda p: remote(VAL, "t", vbuf.at[t], vbuf.at[t], p).start())

    each("z", lambda p: arrived(TZ, "z", tz_v, p))
    each("y", lambda p: arrived(TY, "y", ty_v, p))
    to_z = pltpu.make_async_copy(tz_v, tz_s, loc.at[0])
    to_y = pltpu.make_async_copy(ty_v, ty_s, loc.at[1])
    to_z.start()
    to_y.start()
    all_ten[y] = tz_v[...]
    to_z.wait()
    to_y.wait()
    each("z", lambda p: arrived(AZ, "z", row1, p))

    def pick1(p, to):
        for k in range(nb):
            to[k] = row1[lax.rem(ty_s[p, 0, k], nz)]

    def send1(p):
        pick1(p, s1.at[p])
        remote(SY, "y", s1.at[p], r1.at[y], p).start()

    peers("y", send1)
    pick1(y, r1.at[y])
    each("y", lambda p: arrived(AY, "y", col2, p))

    def pick2(p, to):
        for k in range(nb):
            to[k] = col2[lax.div(tz_s[p, 0, k], nz)]

    def send2(p):
        pick2(p, s2.at[p])
        remote(SZ, "z", s2.at[p], r2.at[z], p).start()

    peers("z", send2)
    pick2(z, r2.at[z])
    peers("y", lambda p: remote(CNT, "y", tz_v, all_ten.at[y], p).start())

    local[3].wait()
    local[5].wait()
    each("y", lambda p: arrived(SY, "y", r1, p))
    each("z", lambda p: arrived(SZ, "z", r2, p))

    first_at, second_at, up_at = [], [], []
    for k in range(nb):
        tenant = ten_s[k]
        part1 = r1[lax.div(tenant, nz), k]
        at2 = r2[lax.rem(tenant, nz), k]
        at1, up = part1[:, :first], part1[:, first:]
        first_at.append(at1)
        second_at.append(at2)
        up_at.append(up)
        span = pl.ds(k * BLOCK, BLOCK)
        low = nt_dot(at1, xv[span, :first]) + nt_dot(at2, xv[span, first:])
        grad = ADAPTER_SCALE * nt_dot(up, vbuf[t, span, :])
        pbuf[t, :rank, span] = low.astype(BF16)
        pbuf[t, rank:, span] = grad.astype(BF16)
    peers("t", lambda p: remote(RANK, "t", pbuf.at[t], pbuf.at[t], p).start())
    each("t", lambda p: arrived(RANK, "t", pbuf, p))
    total = pbuf[0].astype(F32)
    for j in range(1, nt):
        total = total + pbuf[j].astype(F32)
    low_t, grad_t = total[:rank].astype(BF16), total[rank:].astype(BF16)

    for k in range(nb):
        span = slice(k * BLOCK, (k + 1) * BLOCK)
        low_k, grad_k = low_t[:, span], grad_t[:, span]
        g1[k, :, :first] = jnp.dot(grad_k, xv[span, :first], preferred_element_type=F32).astype(BF16)
        g1[k, :, first:] = (
            ADAPTER_SCALE * jnp.dot(low_k, vbuf[t, span, :], preferred_element_type=F32)
        ).astype(BF16)
        g2[k] = jnp.dot(grad_k, xv[span, first:], preferred_element_type=F32).astype(BF16)
    peers("z", lambda p: remote(GZ, "z", g1, gz_v.at[z], p).start())
    peers("y", lambda p: remote(GY, "y", g2, gy_v.at[y], p).start())
    gz_v[z] = g1[...]
    gy_v[y] = g2[...]

    def base_of(p):
        return jnp.dot(xv[...], wbuf[p], preferred_element_type=F32).astype(BF16)

    ebuf[t] = base_of(t)

    def send_base(p):
        arrived(WGT, "t", wbuf, p)
        bsend[p] = base_of(p)
        remote(BASE, "t", bsend.at[p], ebuf.at[t], p).start()

    each("t", send_base)

    each("t", lambda p: arrived(VAL, "t", vbuf, p))
    tiles = 4
    width = feats // tiles
    for i in range(tiles):
        cols = slice(i * width, (i + 1) * width)
        acc = nt_dot(vbuf[0], wbuf[0, cols, :])
        for j in range(1, nt):
            acc = acc + nt_dot(vbuf[j], wbuf[j, cols, :])
        for k in range(nb):
            span = slice(k * BLOCK, (k + 1) * BLOCK)
            if (i + 1) * width <= first:
                at = first_at[k][:, cols]
            else:
                at = second_at[k][:, i * width - first : (i + 1) * width - first]
            gin_v[span, cols] = (acc[span] + tn_dot(grad_t[:, span], at)).astype(BF16)
    gin_copy = pltpu.make_async_copy(gin_v, gin_hbm, loc.at[2])
    gin_copy.start()

    each("z", lambda p: arrived(GZ, "z", gz_v, p))

    def sum1(p, to):
        owner = p * nz + z
        acc = jnp.zeros(g1.shape[1:], F32)
        for j in range(nz):
            for k in range(nb):
                hit = jnp.where(tz_s[j, 0, k] == owner, 1.0, 0.0).astype(F32)
                acc = acc + hit * gz_v[j, k].astype(F32)
        to[...] = acc.astype(BF16)

    def send_sum1(p):
        sum1(p, h1.at[p])
        remote(HY, "y", h1.at[p], hz1.at[y], p).start()

    each("y", send_sum1)
    sum1(y, hz1.at[y])
    each("y", lambda p: arrived(GY, "y", gy_v, p))

    def sum2(p, to):
        owner = y * nz + p
        acc = jnp.zeros(g2.shape[1:], F32)
        for j in range(ny):
            for k in range(nb):
                hit = jnp.where(ty_s[j, 0, k] == owner, 1.0, 0.0).astype(F32)
                acc = acc + hit * gy_v[j, k].astype(F32)
        to[...] = acc.astype(BF16)

    def send_sum2(p):
        sum2(p, h2.at[p])
        remote(HZ, "z", h2.at[p], hz2.at[z], p).start()

    each("z", send_sum2)
    sum2(z, hz2.at[z])

    each("t", lambda p: arrived(BASE, "t", ebuf, p))
    base = ebuf[0].astype(F32)
    for j in range(1, nt):
        base = base + ebuf[j].astype(F32)
    for k in range(nb):
        span = slice(k * BLOCK, (k + 1) * BLOCK)
        raised = tn_dot(low_t[:, span], up_at[k])
        out_ref[span, :] = (base[span] + ADAPTER_SCALE * raised).astype(BF16)

    each("y", lambda p: arrived(CNT, "y", all_ten, p))
    hits = jnp.where(all_ten[:, :, 0, :] == d, 1.0, 0.0).astype(F32)
    count = jnp.sum(hits) * BLOCK
    quota = jnp.full((8, 128), quo_s[d], jnp.int32).astype(F32)
    scale = (quota / jnp.maximum(jnp.full((8, 128), count, F32), 1.0))[:1, :1]
    each("y", lambda p: arrived(HY, "y", hz1, p))
    acc = hz1[0].astype(F32)
    for j in range(1, ny):
        acc = acc + hz1[j].astype(F32)
    da_ref[:, :first] = acc[:, :first] * scale
    db_ref[...] = acc[:, first:] * scale
    each("z", lambda p: arrived(HZ, "z", hz2, p))
    acc = hz2[0].astype(F32)
    for j in range(1, nz):
        acc = acc + hz2[j].astype(F32)
    da_ref[:, first:] = acc * scale

    def left(kind, line, src, dst_buf):
        each(line, lambda p: remote(kind, line, src(p), dst_buf.at[lines[line][0]], p).wait_send())

    left(TZ, "z", lambda p: tile, tz_v)
    left(TY, "y", lambda p: tile, ty_v)
    left(AZ, "z", lambda p: a1, row1)
    left(AY, "y", lambda p: a2, col2)
    left(WGT, "t", lambda p: w_hbm.at[pl.ds(p * feats, feats)], wbuf)
    left(VAL, "t", lambda p: vbuf.at[t], vbuf)
    left(SY, "y", lambda p: s1.at[p], r1)
    left(SZ, "z", lambda p: s2.at[p], r2)
    left(CNT, "y", lambda p: tz_v, all_ten)
    left(RANK, "t", lambda p: pbuf.at[t], pbuf)
    left(GZ, "z", lambda p: g1, gz_v)
    left(GY, "y", lambda p: g2, gy_v)
    left(BASE, "t", lambda p: bsend.at[p], ebuf)
    left(HY, "y", lambda p: h1.at[p], hz1)
    left(HZ, "z", lambda p: h2.at[p], hz2)
    gin_copy.wait()


def solution(mesh):
    nt = mesh.shape["tensor"]
    nz = LINE
    ny = mesh.shape["dp"] // nz

    def on_device(x, w, a, b, v, tenants, quotas):
        rows, feats = x.shape
        values = v.shape[1]
        _, rank, _ = b.shape
        nb = tenants.shape[0]
        first = feats // 2
        wide, half = first + values, feats - first
        most = max(nt, ny, nz)
        hbm = pl.BlockSpec(memory_space=pl.ANY)
        smem = pl.BlockSpec(memory_space=pltpu.SMEM)
        vmem = pl.BlockSpec(memory_space=pltpu.VMEM)
        out, gin, da, db = pl.pallas_call(
            functools.partial(kernel, nt, ny, nz),
            out_shape=(
                jax.ShapeDtypeStruct((rows, values), BF16),
                jax.ShapeDtypeStruct((rows, feats), BF16),
                jax.ShapeDtypeStruct((rank, feats), F32),
                jax.ShapeDtypeStruct((rank, values), F32),
            ),
            in_specs=[smem, smem, hbm, hbm, hbm, hbm, hbm],
            out_specs=(vmem, hbm, vmem, vmem),
            scratch_shapes=[
                pltpu.VMEM((8, 128), jnp.int32),
                pltpu.VMEM((nz, 8, 128), jnp.int32),
                pltpu.VMEM((ny, 8, 128), jnp.int32),
                pltpu.SMEM((nz, 8, 128), jnp.int32),
                pltpu.SMEM((ny, 8, 128), jnp.int32),
                pltpu.VMEM((ny, nz, 8, 128), jnp.int32),
                pltpu.VMEM((rows, feats), BF16),
                pltpu.VMEM((rank, wide), BF16),
                pltpu.VMEM((rank, half), BF16),
                pltpu.VMEM((nz, rank, wide), BF16),
                pltpu.VMEM((ny, rank, half), BF16),
                pltpu.VMEM((ny, nb, rank, wide), BF16),
                pltpu.VMEM((nz, nb, rank, half), BF16),
                pltpu.VMEM((ny, nb, rank, wide), BF16),
                pltpu.VMEM((nz, nb, rank, half), BF16),
                pltpu.VMEM((nt, rows, values), BF16),
                pltpu.VMEM((nt, feats, values), BF16),
                pltpu.VMEM((nt, 2 * rank, rows), BF16),
                pltpu.VMEM((nt, rows, values), BF16),
                pltpu.VMEM((nt, rows, values), BF16),
                pltpu.VMEM((nb, rank, wide), BF16),
                pltpu.VMEM((nb, rank, half), BF16),
                pltpu.VMEM((nz, nb, rank, wide), BF16),
                pltpu.VMEM((ny, nb, rank, half), BF16),
                pltpu.VMEM((ny, rank, wide), BF16),
                pltpu.VMEM((nz, rank, half), BF16),
                pltpu.VMEM((ny, rank, wide), BF16),
                pltpu.VMEM((nz, rank, half), BF16),
                pltpu.VMEM((rows, feats), BF16),
                pltpu.SemaphoreType.DMA((6,)),
                pltpu.SemaphoreType.DMA((15, most)),
                pltpu.SemaphoreType.DMA((15, most)),
            ],
            compiler_params=pltpu.CompilerParams(
                collective_id=0, has_side_effects=True, vmem_limit_bytes=32 << 20
            ),
        )(tenants, quotas, x, w, jnp.swapaxes(a[0], 0, 1), b[0], v)
        return out, gin, jnp.swapaxes(da, 0, 1)[None], db[None]

    return jax.shard_map(
        on_device,
        mesh=mesh,
        in_specs=(
            P("dp", "tensor"),
            P(None, "tensor"),
            P("dp", "tensor", None),
            P("dp", None, "tensor"),
            P("dp", "tensor"),
            P("dp"),
            P(),
        ),
        out_specs=(
            P("dp", "tensor"),
            P("dp", "tensor"),
            P("dp", "tensor", None),
            P("dp", None, "tensor"),
        ),
        check_vma=False,
    )
```

```python
import functools

import jax
import jax.numpy as jnp
from jax import lax
from jax.experimental import pallas as pl
from jax.experimental.pallas import tpu as pltpu
from jax.sharding import PartitionSpec as P

MESH = pl.DeviceIdType.MESH
BLOCK = 128
LINE = 8
ADAPTER_SCALE = 2.0
BF16 = jnp.bfloat16
F32 = jnp.float32

TZ, TY, AZ, AY, SY, SZ, VAL, FWD, WGT, RANK, PRE, BASE, GZ, GY, HY, HZ, CNT = range(17)


def far_first(n):
    return sorted(range(1, n), key=lambda off: (-min(off, n - off), off))


def nt_dot(a, b):
    return lax.dot_general(a, b, (((1,), (1,)), ((), ())), preferred_element_type=F32)


def tn_dot(a, b):
    return lax.dot_general(a, b, (((0,), (0,)), ((), ())), preferred_element_type=F32)


def kernel(
    nt, ny, nz,
    ten_hbm, quo_hbm, x_hbm, w_hbm, a_hbm, b_hbm, v_hbm,
    out_ref, gin_v, da_ref, db_ref,
    ten_s, quo_s, tile, tz_v, ty_v, tz_s, ty_s, all_ten,
    xv, a1, a2, row1, col2, s1, s2, r1, r2,
    vbuf, wbuf, pbuf, presend, prebuf, keep, bsend, ebuf, g1, g2, gz_v, gy_v, h1, h2, hz1, hz2,
    loc, ss, rs,
):
    t = lax.axis_index("tensor")
    d = lax.axis_index("dp")
    y, z = lax.div(d, nz), lax.rem(d, nz)
    nx = nt // 2
    x, core = lax.div(t, 2), lax.rem(t, 2)
    twin = t + 1 - 2 * core
    rows, feats = xv.shape
    nb = rows // BLOCK
    half = a2.shape[1]
    first = feats - half
    values = v_hbm.shape[1]
    rank = a2.shape[0]

    lines = {
        "t": (t, nt, lambda p: {"tensor": p}),
        "y": (y, ny, lambda p: {"dp": p * nz + z}),
        "z": (z, nz, lambda p: {"dp": y * nz + p}),
    }

    def remote(kind, line, src, dst, peer):
        me, _, dev = lines[line]
        return pltpu.make_async_remote_copy(
            src_ref=src, dst_ref=dst, send_sem=ss.at[kind, peer], recv_sem=rs.at[kind, me],
            device_id=dev(peer), device_id_type=MESH,
        )

    def arrived(kind, line, buf, peer):
        _, _, dev = lines[line]
        pltpu.make_async_remote_copy(
            src_ref=buf.at[peer], dst_ref=buf.at[peer], send_sem=ss.at[kind, peer],
            recv_sem=rs.at[kind, peer], device_id=dev(peer), device_id_type=MESH,
        ).wait_recv()

    def peers(line, fn):
        me, n, _ = lines[line]
        for off in far_first(n):
            fn(lax.rem(me + off, n))

    def each(line, fn):
        me, n, _ = lines[line]

        def body(off, carry):
            fn(lax.rem(me + off, n))
            return carry

        lax.fori_loop(1, n, body, 0)

    barrier = pltpu.get_barrier_semaphore()
    for line in ("t", "y", "z"):
        dev = lines[line][2]
        each(line, lambda p: pl.semaphore_signal(barrier, inc=1, device_id=dev(p), device_id_type=MESH))
    local = [
        pltpu.make_async_copy(a_hbm.at[:, pl.ds(0, first)], a1.at[:, pl.ds(0, first)], loc.at[0]),
        pltpu.make_async_copy(b_hbm, a1.at[:, pl.ds(first, values)], loc.at[1]),
        pltpu.make_async_copy(a_hbm.at[:, pl.ds(first, half)], a2, loc.at[2]),
        pltpu.make_async_copy(ten_hbm, ten_s, loc.at[6]),
        pltpu.make_async_copy(v_hbm, vbuf.at[t], loc.at[4]),
        pltpu.make_async_copy(x_hbm, xv, loc.at[3]),
        pltpu.make_async_copy(w_hbm.at[pl.ds(t * feats, feats)], wbuf.at[t], loc.at[5]),
        pltpu.make_async_copy(quo_hbm, quo_s, loc.at[7]),
    ]
    for copy in local:
        copy.start()
    get_a, get_b, get_a2, get_ten, get_v, get_x, get_w, get_quo = local
    get_ten.wait()
    lane = lax.broadcasted_iota(jnp.int32, tile.shape, 1)
    mine = jnp.full(tile.shape, -1, jnp.int32)
    for k in range(nb):
        mine = jnp.where(lane == k, ten_s[k], mine)
    tile[...] = mine
    tz_v[z] = mine
    ty_v[y] = mine
    get_a.wait()
    get_b.wait()
    get_a2.wait()
    row1[z] = a1[...]
    col2[y] = a2[...]
    get_v.wait()
    pl.semaphore_wait(barrier, nt + ny + nz - 3)

    peers("z", lambda p: remote(TZ, "z", tile, tz_v.at[z], p).start())
    peers("y", lambda p: remote(TY, "y", tile, ty_v.at[y], p).start())
    peers("z", lambda p: remote(AZ, "z", a1, row1.at[z], p).start())
    peers("y", lambda p: remote(AY, "y", a2, col2.at[y], p).start())

    near = [off for off in range(1, nx) if min(off, nx - off) == 1]
    far = [off for off in range(1, nx) if off not in near]

    def chip(off):
        return lax.rem(x + off, nx)

    def value_to(p):
        return remote(VAL, "t", vbuf.at[t], vbuf.at[t], p)

    def weight_to(p):
        return remote(WGT, "t", w_hbm.at[pl.ds(p * feats, feats)], wbuf.at[t], p)

    for off in far + near:
        value_to(2 * chip(off) + core).start()
    value_to(twin).start()
    weight_to(twin).start()
    for off in near:
        weight_to(2 * chip(off) + core).start()
        weight_to(2 * chip(off) + 1 - core).start()

    each("z", lambda p: arrived(TZ, "z", tz_v, p))
    each("y", lambda p: arrived(TY, "y", ty_v, p))
    to_z = pltpu.make_async_copy(tz_v, tz_s, loc.at[0])
    to_y = pltpu.make_async_copy(ty_v, ty_s, loc.at[1])
    to_z.start()
    to_y.start()
    all_ten[y] = tz_v[...]
    to_z.wait()
    to_y.wait()
    each("z", lambda p: arrived(AZ, "z", row1, p))

    def pick1(p, to):
        for k in range(nb):
            to[k] = row1[lax.rem(ty_s[p, 0, k], nz)]

    def send1(p):
        pick1(p, s1.at[p])
        remote(SY, "y", s1.at[p], r1.at[y], p).start()

    peers("y", send1)
    pick1(y, r1.at[y])
    each("y", lambda p: arrived(AY, "y", col2, p))

    def pick2(p, to):
        for k in range(nb):
            to[k] = col2[lax.div(tz_s[p, 0, k], nz)]

    def send2(p):
        pick2(p, s2.at[p])
        remote(SZ, "z", s2.at[p], r2.at[z], p).start()

    peers("z", send2)
    pick2(z, r2.at[z])
    peers("y", lambda p: remote(CNT, "y", tz_v, all_ten.at[y], p).start())

    def forward(p):
        return pltpu.make_async_remote_copy(
            src_ref=vbuf.at[p], dst_ref=vbuf.at[p], send_sem=ss.at[FWD, p], recv_sem=rs.at[VAL, p],
            device_id={"tensor": twin}, device_id_type=MESH,
        )

    for off in far + near:
        p = 2 * chip(off) + core
        arrived(VAL, "t", vbuf, p)
        forward(p).start()

    def base_of(p):
        return jnp.dot(xv[...], wbuf[p], preferred_element_type=F32)

    def pre_to(q):
        return pltpu.make_async_remote_copy(
            src_ref=presend.at[q], dst_ref=prebuf.at[q], send_sem=ss.at[PRE, q], recv_sem=rs.at[PRE, q],
            device_id={"tensor": twin}, device_id_type=MESH,
        )

    def halves(q):
        presend[q] = base_of(2 * q + 1 - core).astype(BF16)
        pre_to(q).start()
        keep[q] = base_of(2 * q + core)

    def both(q):
        pre_to(q).wait_recv()
        return keep[q] + prebuf[q].astype(F32)

    def base_to(q):
        return pltpu.make_async_remote_copy(
            src_ref=bsend.at[q], dst_ref=ebuf.at[x], send_sem=ss.at[BASE, q], recv_sem=rs.at[BASE, x],
            device_id={"tensor": 2 * q + core}, device_id_type=MESH,
        )

    def base_from(q):
        pltpu.make_async_remote_copy(
            src_ref=bsend.at[q], dst_ref=ebuf.at[q], send_sem=ss.at[BASE, q], recv_sem=rs.at[BASE, q],
            device_id={"tensor": 2 * q + core}, device_id_type=MESH,
        ).wait_recv()

    def send_base(q):
        bsend[q] = both(q).astype(BF16)
        base_to(q).start()

    get_x.wait()
    get_w.wait()
    arrived(WGT, "t", wbuf, twin)
    halves(x)

    each("y", lambda p: arrived(SY, "y", r1, p))
    each("z", lambda p: arrived(SZ, "z", r2, p))

    first_at, second_at, up_at = [], [], []
    for k in range(nb):
        tenant = ten_s[k]
        part1 = r1[lax.div(tenant, nz), k]
        at2 = r2[lax.rem(tenant, nz), k]
        at1, up = part1[:, :first], part1[:, first:]
        first_at.append(at1)
        second_at.append(at2)
        up_at.append(up)
        span = pl.ds(k * BLOCK, BLOCK)
        low = nt_dot(at1, xv[span, :first]) + nt_dot(at2, xv[span, first:])
        grad = ADAPTER_SCALE * nt_dot(up, vbuf[t, span, :])
        pbuf[t, :rank, span] = low.astype(BF16)
        pbuf[t, rank:, span] = grad.astype(BF16)
    peers("t", lambda p: remote(RANK, "t", pbuf.at[t], pbuf.at[t], p).start())
    for off in far:
        weight_to(2 * chip(off) + core).start()
        weight_to(2 * chip(off) + 1 - core).start()
    for off in near:
        arrived(WGT, "t", wbuf, 2 * chip(off) + core)
        arrived(WGT, "t", wbuf, 2 * chip(off) + 1 - core)
        halves(chip(off))
    each("t", lambda p: arrived(RANK, "t", pbuf, p))
    total = pbuf[0].astype(F32)
    for j in range(1, nt):
        total = total + pbuf[j].astype(F32)
    low_t, grad_t = total[:rank].astype(BF16), total[rank:].astype(BF16)

    for k in range(nb):
        span = slice(k * BLOCK, (k + 1) * BLOCK)
        low_k, grad_k = low_t[:, span], grad_t[:, span]
        g1[k, :, :first] = jnp.dot(grad_k, xv[span, :first], preferred_element_type=F32).astype(BF16)
        g1[k, :, first:] = (
            ADAPTER_SCALE * jnp.dot(low_k, vbuf[t, span, :], preferred_element_type=F32)
        ).astype(BF16)
        g2[k] = jnp.dot(grad_k, xv[span, first:], preferred_element_type=F32).astype(BF16)
    peers("z", lambda p: remote(GZ, "z", g1, gz_v.at[z], p).start())
    peers("y", lambda p: remote(GY, "y", g2, gy_v.at[y], p).start())
    gz_v[z] = g1[...]
    gy_v[y] = g2[...]

    def left(kind, line, src, dst_buf):
        each(line, lambda p: remote(kind, line, src(p), dst_buf.at[lines[line][0]], p).wait_send())

    for off in near:
        send_base(chip(off))
    left(TZ, "z", lambda p: tile, tz_v)
    left(TY, "y", lambda p: tile, ty_v)
    left(AZ, "z", lambda p: a1, row1)
    left(AY, "y", lambda p: a2, col2)
    left(SY, "y", lambda p: s1.at[p], r1)
    left(SZ, "z", lambda p: s2.at[p], r2)
    left(CNT, "y", lambda p: tz_v, all_ten)
    left(RANK, "t", lambda p: pbuf.at[t], pbuf)
    for off in far + near:
        value_to(2 * chip(off) + core).wait_send()
        forward(2 * chip(off) + core).wait_send()
    value_to(twin).wait_send()

    for off in far:
        arrived(WGT, "t", wbuf, 2 * chip(off) + core)
        arrived(WGT, "t", wbuf, 2 * chip(off) + 1 - core)
        halves(chip(off))

    each("z", lambda p: arrived(GZ, "z", gz_v, p))

    def sum1(p, to):
        owner = p * nz + z
        acc = jnp.zeros(g1.shape[1:], F32)
        for j in range(nz):
            for k in range(nb):
                hit = jnp.where(tz_s[j, 0, k] == owner, 1.0, 0.0).astype(F32)
                acc = acc + hit * gz_v[j, k].astype(F32)
        to[...] = acc.astype(BF16)

    def send_sum1(p):
        sum1(p, h1.at[p])
        remote(HY, "y", h1.at[p], hz1.at[y], p).start()

    each("y", send_sum1)
    for off in far:
        send_base(chip(off))
    sum1(y, hz1.at[y])
    each("y", lambda p: arrived(GY, "y", gy_v, p))

    def sum2(p, to):
        owner = y * nz + p
        acc = jnp.zeros(g2.shape[1:], F32)
        for j in range(ny):
            for k in range(nb):
                hit = jnp.where(ty_s[j, 0, k] == owner, 1.0, 0.0).astype(F32)
                acc = acc + hit * gy_v[j, k].astype(F32)
        to[...] = acc.astype(BF16)

    def send_sum2(p):
        sum2(p, h2.at[p])
        remote(HZ, "z", h2.at[p], hz2.at[z], p).start()

    each("z", send_sum2)
    sum2(z, hz2.at[z])

    arrived(VAL, "t", vbuf, twin)
    for off in far + near:
        arrived(VAL, "t", vbuf, 2 * chip(off) + 1 - core)
    tiles = 4
    width = feats // tiles
    for i in range(tiles):
        cols = slice(i * width, (i + 1) * width)
        acc = nt_dot(vbuf[0], wbuf[0, cols, :])
        for j in range(1, nt):
            acc = acc + nt_dot(vbuf[j], wbuf[j, cols, :])
        for k in range(nb):
            span = slice(k * BLOCK, (k + 1) * BLOCK)
            if (i + 1) * width <= first:
                at = first_at[k][:, cols]
            else:
                at = second_at[k][:, i * width - first : (i + 1) * width - first]
            gin_v[span, cols] = (acc[span] + tn_dot(grad_t[:, span], at)).astype(BF16)

    base = both(x)
    for off in near + far:
        base_from(chip(off))
        base = base + ebuf[chip(off)].astype(F32)
    for k in range(nb):
        span = slice(k * BLOCK, (k + 1) * BLOCK)
        raised = tn_dot(low_t[:, span], up_at[k])
        out_ref[span, :] = (base[span] + ADAPTER_SCALE * raised).astype(BF16)

    each("y", lambda p: arrived(CNT, "y", all_ten, p))
    get_quo.wait()
    hits = jnp.where(all_ten[:, :, 0, :] == d, 1.0, 0.0).astype(F32)
    count = jnp.sum(hits) * BLOCK
    quota = jnp.full((8, 128), quo_s[d], jnp.int32).astype(F32)
    scale = (quota / jnp.maximum(jnp.full((8, 128), count, F32), 1.0))[:1, :1]
    each("y", lambda p: arrived(HY, "y", hz1, p))
    acc = hz1[0].astype(F32)
    for j in range(1, ny):
        acc = acc + hz1[j].astype(F32)
    da_ref[:, :first] = acc[:, :first] * scale
    db_ref[...] = acc[:, first:] * scale
    each("z", lambda p: arrived(HZ, "z", hz2, p))
    acc = hz2[0].astype(F32)
    for j in range(1, nz):
        acc = acc + hz2[j].astype(F32)
    da_ref[:, first:] = acc * scale

    weight_to(twin).wait_send()
    for off in far + near:
        weight_to(2 * chip(off) + core).wait_send()
        weight_to(2 * chip(off) + 1 - core).wait_send()
        base_to(chip(off)).wait_send()
        pre_to(chip(off)).wait_send()
    pre_to(x).wait_send()
    left(GZ, "z", lambda p: g1, gz_v)
    left(GY, "y", lambda p: g2, gy_v)
    left(HY, "y", lambda p: h1.at[p], hz1)
    left(HZ, "z", lambda p: h2.at[p], hz2)


def write_out(out_v, gin_v, da_v, db_v, out_hbm, gin_hbm, da_hbm, db_hbm, sems):
    pairs = ((gin_v, gin_hbm), (out_v, out_hbm), (da_v, da_hbm), (db_v, db_hbm))
    copies = [pltpu.make_async_copy(a, b, sems.at[i]) for i, (a, b) in enumerate(pairs)]
    for copy in copies:
        copy.start()
    for copy in copies:
        copy.wait()


def solution(mesh):
    nt = mesh.shape["tensor"]
    nz = LINE
    ny = mesh.shape["dp"] // nz

    def on_device(x, w, a, b, v, tenants, quotas):
        rows, feats = x.shape
        values = v.shape[1]
        _, rank, _ = b.shape
        nb = tenants.shape[0]
        first = feats // 2
        wide, half = first + values, feats - first
        most = max(nt, ny, nz)
        hbm = pl.BlockSpec(memory_space=pltpu.MemorySpace.HBM)
        anywhere = pl.BlockSpec(memory_space=pl.ANY)
        vmem = pl.BlockSpec(memory_space=pltpu.VMEM)
        out, gin, da, db = pl.pallas_call(
            functools.partial(kernel, nt, ny, nz),
            out_shape=(
                jax.ShapeDtypeStruct((rows, values), BF16),
                jax.ShapeDtypeStruct((rows, feats), BF16),
                jax.ShapeDtypeStruct((rank, feats), F32),
                jax.ShapeDtypeStruct((rank, values), F32),
            ),
            in_specs=[hbm] * 7,
            out_specs=(vmem,) * 4,
            scratch_shapes=[
                pltpu.SMEM((nb,), jnp.int32),
                pltpu.SMEM(quotas.shape, jnp.int32),
                pltpu.VMEM((8, 128), jnp.int32),
                pltpu.VMEM((nz, 8, 128), jnp.int32),
                pltpu.VMEM((ny, 8, 128), jnp.int32),
                pltpu.SMEM((nz, 8, 128), jnp.int32),
                pltpu.SMEM((ny, 8, 128), jnp.int32),
                pltpu.VMEM((ny, nz, 8, 128), jnp.int32),
                pltpu.VMEM((rows, feats), BF16),
                pltpu.VMEM((rank, wide), BF16),
                pltpu.VMEM((rank, half), BF16),
                pltpu.VMEM((nz, rank, wide), BF16),
                pltpu.VMEM((ny, rank, half), BF16),
                pltpu.VMEM((ny, nb, rank, wide), BF16),
                pltpu.VMEM((nz, nb, rank, half), BF16),
                pltpu.VMEM((ny, nb, rank, wide), BF16),
                pltpu.VMEM((nz, nb, rank, half), BF16),
                pltpu.VMEM((nt, rows, values), BF16),
                pltpu.VMEM((nt, feats, values), BF16),
                pltpu.VMEM((nt, 2 * rank, rows), BF16),
                pltpu.VMEM((nt // 2, rows, values), BF16),
                pltpu.VMEM((nt // 2, rows, values), BF16),
                pltpu.VMEM((nt // 2, rows, values), F32),
                pltpu.VMEM((nt // 2, rows, values), BF16),
                pltpu.VMEM((nt // 2, rows, values), BF16),
                pltpu.VMEM((nb, rank, wide), BF16),
                pltpu.VMEM((nb, rank, half), BF16),
                pltpu.VMEM((nz, nb, rank, wide), BF16),
                pltpu.VMEM((ny, nb, rank, half), BF16),
                pltpu.VMEM((ny, rank, wide), BF16),
                pltpu.VMEM((nz, rank, half), BF16),
                pltpu.VMEM((ny, rank, wide), BF16),
                pltpu.VMEM((nz, rank, half), BF16),
                pltpu.SemaphoreType.DMA((8,)),
                pltpu.SemaphoreType.DMA((17, most)),
                pltpu.SemaphoreType.DMA((17, most)),
            ],
            compiler_params=pltpu.CompilerParams(
                collective_id=0, has_side_effects=True, vmem_limit_bytes=48 << 20
            ),
        )(*[
            pltpu.with_memory_space_constraint(arg, pltpu.MemorySpace.HBM)
            for arg in (tenants, quotas, x, w, jnp.swapaxes(a[0], 0, 1), b[0], v)
        ])
        out, gin, da, db = pl.pallas_call(
            write_out,
            out_shape=(
                jax.ShapeDtypeStruct((rows, values), BF16),
                jax.ShapeDtypeStruct((rows, feats), BF16),
                jax.ShapeDtypeStruct((rank, feats), F32),
                jax.ShapeDtypeStruct((rank, values), F32),
            ),
            in_specs=[anywhere] * 4,
            out_specs=(hbm,) * 4,
            scratch_shapes=[pltpu.SemaphoreType.DMA((4,))],
            compiler_params=pltpu.CompilerParams(vmem_limit_bytes=4 << 20),
        )(out, gin, da, db)
        return out, gin, jnp.swapaxes(da, 0, 1)[None], db[None]

    return jax.shard_map(
        on_device,
        mesh=mesh,
        in_specs=(
            P("dp", "tensor"),
            P(None, "tensor"),
            P("dp", "tensor", None),
            P("dp", None, "tensor"),
            P("dp", "tensor"),
            P("dp"),
            P(),
        ),
        out_specs=(
            P("dp", "tensor"),
            P("dp", "tensor"),
            P("dp", "tensor", None),
            P("dp", None, "tensor"),
        ),
        check_vma=False,
    )
```

```python
import functools

import jax
import jax.numpy as jnp
from jax import lax
from jax.experimental import pallas as pl
from jax.experimental.pallas import tpu as pltpu
from jax.sharding import PartitionSpec as P

MESH = pl.DeviceIdType.MESH
BLOCK = 128
LINE = 8
ADAPTER_SCALE = 2.0
BF16 = jnp.bfloat16
F32 = jnp.float32

TZ, TY, AZ, AY, VAL, FWD, BASE, HY, HZ, CNT, SY, SZ, RANK, GZ, GY, WGT, PRE, SHARE, SY2, SZ2 = range(20)
SECOND = 10
KINDS = SECOND + GY + 1


def far_first(n):
    return sorted(range(1, n), key=lambda off: (-min(off, n - off), off))


def nt_dot(a, b):
    return lax.dot_general(a, b, (((1,), (1,)), ((), ())), preferred_element_type=F32)


def tn_dot(a, b):
    return lax.dot_general(a, b, (((0,), (0,)), ((), ())), preferred_element_type=F32)


def kernel(
    nt, ny, nz,
    ten_hbm, quo_hbm, x_hbm, w_hbm, a_hbm, b_hbm, v_hbm,
    out_hbm, gin_hbm, da_hbm, db_hbm,
    out_v, gin_v, da_v, db_v, ten_s, quo_s, tile, tz_v, ty_v, tz_s, ty_s, all_ten,
    xv, row1, col2, s1, s2, r1_first, r1_second, r2_first, r2_second,
    vbuf, wbuf, pbuf, presend, prebuf, keep, bsend, ebuf, g1, g2, gz_v, gy_v, acc1, acc2, h1, h2, hz1, hz2, gin_acc,
    loc, ss, rs, wgt_rs, pre_rs,
):
    t = lax.axis_index("tensor")
    d = lax.axis_index("dp")
    y, z = lax.div(d, nz), lax.rem(d, nz)
    nx = nt // 2
    x, core = lax.div(t, 2), lax.rem(t, 2)
    twin = t + 1 - 2 * core
    rows, feats = xv.shape
    nb = rows // BLOCK
    rank, half = col2.shape[1:]
    r1, r2 = (r1_first, r1_second), (r2_first, r2_second)
    first = feats - half
    values = v_hbm.shape[1]

    lines = {
        "t": (t, nt, lambda p: {"tensor": p}),
        "y": (y, ny, lambda p: {"dp": p * nz + z}),
        "z": (z, nz, lambda p: {"dp": y * nz + p}),
    }

    def remote(kind, line, src, dst, peer, recv=None):
        return pltpu.make_async_remote_copy(
            src_ref=src, dst_ref=dst, send_sem=ss.at[kind], recv_sem=rs.at[kind] if recv is None else recv,
            device_id=lines[line][2](peer), device_id_type=MESH,
        )

    def all_of(line, buf, recv, send=0):
        me, n, dev = lines[line]
        return pltpu.make_async_remote_copy(
            src_ref=buf, dst_ref=buf, send_sem=ss.at[send], recv_sem=recv,
            device_id=dev(lax.rem(me + 1, n)), device_id_type=MESH,
        )

    def arrived(kind, line, buf):
        others = lines[line][1] - 1
        if others:
            all_of(line, buf.at[pl.ds(0, others)], rs.at[kind]).wait_recv()

    def left(kind, line, buf, copies=None):
        others = lines[line][1] - 1 if copies is None else copies
        if others:
            all_of(line, buf.at[pl.ds(0, others)], rs.at[0], kind).wait_send()

    def left_both(kind, line, buf):
        others = lines[line][1] - 1
        if others:
            all_of(line, buf.at[:, pl.ds(0, others)], rs.at[0], kind).wait_send()

    def peers(line, fn):
        me, n, _ = lines[line]
        for off in far_first(n):
            fn(lax.rem(me + off, n))

    def each(line, fn):
        me, n, _ = lines[line]

        def body(off, carry):
            fn(lax.rem(me + off, n))
            return carry

        lax.fori_loop(1, n, body, 0)

    barrier = pltpu.get_barrier_semaphore()
    for line in ("t", "y", "z"):
        dev = lines[line][2]
        each(line, lambda p: pl.semaphore_signal(barrier, inc=1, device_id=dev(p), device_id_type=MESH))
    local = [
        pltpu.make_async_copy(ten_hbm, ten_s, loc.at[0]),
        pltpu.make_async_copy(a_hbm.at[:, pl.ds(0, first)], row1.at[z, :, pl.ds(0, first)], loc.at[1]),
        pltpu.make_async_copy(b_hbm, row1.at[z, :, pl.ds(first, values)], loc.at[2]),
        pltpu.make_async_copy(a_hbm.at[:, pl.ds(first, half)], col2.at[y], loc.at[3]),
        pltpu.make_async_copy(x_hbm, xv, loc.at[4]),
        pltpu.make_async_copy(v_hbm, vbuf.at[t], loc.at[5]),
        pltpu.make_async_copy(w_hbm.at[pl.ds(t * feats, feats)], wbuf.at[t], loc.at[6]),
        pltpu.make_async_copy(quo_hbm, quo_s, loc.at[7]),
    ]
    for copy in local:
        copy.start()
    local[0].wait()
    lane = lax.broadcasted_iota(jnp.int32, tile.shape, 1)
    mine = jnp.full(tile.shape, -1, jnp.int32)
    for k in range(nb):
        mine = jnp.where(lane == k, ten_s[k], mine)
    tile[...] = mine
    tz_v[z] = mine
    ty_v[y] = mine
    pl.semaphore_wait(barrier, nt + ny + nz - 3)

    def adapter_to_z(p):
        remote(AZ, "z", a_hbm.at[:, pl.ds(0, first)], row1.at[z, :, pl.ds(0, first)], p).start()
        remote(AZ, "z", b_hbm, row1.at[z, :, pl.ds(first, values)], p).start()

    peers("z", lambda p: remote(TZ, "z", tile, tz_v.at[z], p).start())
    peers("y", lambda p: remote(TY, "y", tile, ty_v.at[y], p).start())
    peers("z", adapter_to_z)
    peers("y", lambda p: remote(AY, "y", a_hbm.at[:, pl.ds(first, half)], col2.at[y], p).start())

    near = [off for off in range(1, nx) if min(off, nx - off) == 1]
    far = [off for off in range(1, nx) if off not in near]

    def chip(off):
        return lax.rem(x + off, nx)

    def value_to(p):
        return remote(VAL, "t", vbuf.at[t], vbuf.at[t], p)

    def weight_to(p, part=0, parts=1):
        size = feats // parts
        return remote(
            WGT, "t", w_hbm.at[pl.ds(p * feats + part * size, size)],
            wbuf.at[t, pl.ds(part * size, size)], p, wgt_rs.at[t],
        )

    def weight_arrived(p):
        all_of("t", wbuf.at[p], wgt_rs.at[p]).wait_recv()

    def pair(offs):
        return [2 * chip(off) + c for off in offs for c in (core, 1 - core)]

    ways = [(line, step) for line in ("y", "z") for step in (1, -1) if lines[line][1] > 1]
    mine_half = lax.rem(y + z, 2)
    rows_half = feats // 2
    rows_share = rows_half // len(ways)

    def share(p, i):
        line, step = ways[i]
        me, n, _ = lines[line]
        span = pl.ds(mine_half * rows_half + i * rows_share, rows_share)
        return remote(SHARE, line, wbuf.at[p, span], wbuf.at[p, span], lax.rem(me + step + n, n))

    near_weights = pair(near)
    shared = (pair(far), near_weights[::2])
    count_shared = len(shared[0]) + len(shared[1])
    weight_to(twin).start()
    for p in shared[0] + shared[1]:
        weight_to(p, mine_half, 2).start()
    for p in near_weights[1::2]:
        weight_to(p, 0, 4).start()

    arrived(TZ, "z", tz_v)
    arrived(TY, "y", ty_v)
    to_z = pltpu.make_async_copy(tz_v, tz_s, loc.at[0])
    to_y = pltpu.make_async_copy(ty_v, ty_s, loc.at[1])
    to_z.start()
    to_y.start()
    all_ten[y] = tz_v[...]
    to_z.wait()
    to_y.wait()
    for copy in local[1:4]:
        copy.wait()

    def pick1(k, p):
        return row1[lax.rem(ty_s[p, 0, k], nz)]

    def pick2(k, p):
        return col2[lax.div(tz_s[p, 0, k], nz)]

    def send1(k, p):
        s1[k, p] = pick1(k, p)
        kind, recv = (SY if k == 0 else SY2), rs.at[SY + k * SECOND]
        remote(kind, "y", s1.at[k, p], r1[k].at[y], p, recv).start()

    def send2(k, p):
        s2[k, p] = pick2(k, p)
        kind, recv = (SZ if k == 0 else SZ2), rs.at[SZ + k * SECOND]
        remote(kind, "z", s2.at[k, p], r2[k].at[z], p, recv).start()

    arrived(AZ, "z", row1)
    peers("y", lambda p: send1(0, p))
    arrived(AY, "y", col2)
    peers("z", lambda p: send2(0, p))
    for k in range(nb):
        r1[k][y] = pick1(k, y)
        r2[k][z] = pick2(k, z)

    def base_of(p):
        return jnp.dot(xv[...], wbuf[p], preferred_element_type=F32)

    def pre_to(q):
        return pltpu.make_async_remote_copy(
            src_ref=presend.at[q], dst_ref=prebuf.at[q], send_sem=ss.at[PRE], recv_sem=pre_rs.at[q],
            device_id={"tensor": twin}, device_id_type=MESH,
        )

    def halves(q):
        presend[q] = base_of(2 * q + 1 - core).astype(BF16)
        pre_to(q).start()
        keep[q] = base_of(2 * q + core)

    def both(q):
        pre_to(q).wait_recv()
        return keep[q] + prebuf[q].astype(F32)

    def base_to(q):
        return pltpu.make_async_remote_copy(
            src_ref=bsend.at[q], dst_ref=ebuf.at[x], send_sem=ss.at[BASE], recv_sem=rs.at[BASE],
            device_id={"tensor": 2 * q + core}, device_id_type=MESH,
        )

    def send_base(q):
        bsend[q] = both(q).astype(BF16)
        base_to(q).start()

    def forward(p):
        return pltpu.make_async_remote_copy(
            src_ref=vbuf.at[p], dst_ref=vbuf.at[p], send_sem=ss.at[FWD], recv_sem=rs.at[FWD],
            device_id={"tensor": twin}, device_id_type=MESH,
        )

    local[4].wait()
    local[5].wait()
    local[6].wait()
    weight_arrived(twin)
    halves(x)
    left(SY, "y", s1.at[0])
    left(SZ, "z", s2.at[0])

    def send_rest():
        for k in range(1, nb):
            peers("y", lambda p: send1(k, p))
            peers("z", lambda p: send2(k, p))

    pl.when(core == 0)(send_rest)
    for group in shared:
        for p in group:
            all_of("t", wbuf.at[p, pl.ds(0, rows_half)], wgt_rs.at[p]).wait_recv()
        if group is shared[0]:
            pl.when(core == 1)(send_rest)
        for i in range(len(ways)):
            for p in group:
                share(p, i).start()
    peers("y", lambda p: remote(CNT, "y", tz_v, all_ten.at[y], p).start())

    first_at, second_at, up_at = [], [], []

    def rank_products(k):
        arrived(SY + k * SECOND, "y", r1[k])
        arrived(SZ + k * SECOND, "z", r2[k])
        tenant = ten_s[k]
        part1 = r1[k][lax.div(tenant, nz)]
        at2 = r2[k][lax.rem(tenant, nz)]
        at1, up = part1[:, :first], part1[:, first:]
        first_at.append(at1)
        second_at.append(at2)
        up_at.append(up)
        span = pl.ds(k * BLOCK, BLOCK)
        low = nt_dot(at1, xv[span, :first]) + nt_dot(at2, xv[span, first:])
        grad = ADAPTER_SCALE * nt_dot(up, vbuf[t, span, :])
        pbuf[k, t, :rank] = low.astype(BF16)
        pbuf[k, t, rank:] = grad.astype(BF16)
        recv = rs.at[RANK + k * SECOND]
        peers("t", lambda p: remote(RANK, "t", pbuf.at[k, t], pbuf.at[k, t], p, recv).start())

    low_t, grad_t = [], []

    def block_gradients(k):
        arrived(RANK + k * SECOND, "t", pbuf.at[k])
        total = pbuf[k, 0].astype(F32)
        for j in range(1, nt):
            total = total + pbuf[k, j].astype(F32)
        low_k, grad_k = total[:rank].astype(BF16), total[rank:].astype(BF16)
        low_t.append(low_k)
        grad_t.append(grad_k)
        span = slice(k * BLOCK, (k + 1) * BLOCK)
        g1[k, :, :first] = jnp.dot(grad_k, xv[span, :first], preferred_element_type=F32).astype(BF16)
        g1[k, :, first:] = (
            ADAPTER_SCALE * jnp.dot(low_k, vbuf[t, span, :], preferred_element_type=F32)
        ).astype(BF16)
        g2[k] = jnp.dot(grad_k, xv[span, first:], preferred_element_type=F32).astype(BF16)
        recv_z, recv_y = rs.at[GZ + k * SECOND], rs.at[GY + k * SECOND]
        peers("z", lambda p: remote(GZ, "z", g1.at[k], gz_v.at[k, z], p, recv_z).start())
        peers("y", lambda p: remote(GY, "y", g2.at[k], gy_v.at[k, y], p, recv_y).start())
        gz_v[k, z] = g1[k]
        gy_v[k, y] = g2[k]

    rank_products(0)
    for p in near_weights[1::2]:
        weight_to(p, 1, 4).start()
    rank_products(1)
    for part in range(2, 4):
        for p in near_weights[1::2]:
            weight_to(p, part, 4).start()
    for off in far + near:
        value_to(2 * chip(off) + core).start()
    forward(t).start()
    block_gradients(0)
    block_gradients(1)

    if count_shared:
        all_of("t", wbuf.at[pl.ds(0, count_shared), pl.ds(0, rows_half)], rs.at[SHARE]).wait_recv()
    for off in far:
        halves(chip(off))
    for off in far:
        send_base(chip(off))

    def add_up(k, p, owner, ten, buf, acc):
        total = acc[p]
        for j in range(buf.shape[1]):
            hit = jnp.where(ten[j, 0, k] == owner, 1.0, 0.0).astype(F32)
            total = total + hit * buf[k, j].astype(F32)
        return total

    def add1(k, p):
        return add_up(k, p, p * nz + z, tz_s, gz_v, acc1)

    def add2(k, p):
        return add_up(k, p, y * nz + p, ty_s, gy_v, acc2)

    acc1[...] = jnp.zeros_like(acc1)
    acc2[...] = jnp.zeros_like(acc2)
    for k in range(nb - 1):
        arrived(GZ + k * SECOND, "z", gz_v.at[k])
        arrived(GY + k * SECOND, "y", gy_v.at[k])

        def keep1(p, carry):
            acc1[p] = add1(k, p)
            return carry

        def keep2(p, carry):
            acc2[p] = add2(k, p)
            return carry

        lax.fori_loop(0, ny, keep1, 0)
        lax.fori_loop(0, nz, keep2, 0)

    for p in near_weights[1::2]:
        weight_arrived(p)
    for off in near:
        halves(chip(off))
    last = nb - 1

    def send_sum1(p):
        h1[p] = add1(last, p).astype(BF16)
        remote(HY, "y", h1.at[p], hz1.at[y], p).start()

    def send_sum2(p):
        h2[p] = add2(last, p).astype(BF16)
        remote(HZ, "z", h2.at[p], hz2.at[z], p).start()

    arrived(GZ + last * SECOND, "z", gz_v.at[last])
    peers("y", send_sum1)
    arrived(GY + last * SECOND, "y", gy_v.at[last])
    peers("z", send_sum2)
    hz1[y] = add1(last, y).astype(BF16)
    hz2[z] = add2(last, z).astype(BF16)
    for off in near:
        send_base(chip(off))

    if far + near:
        all_of("t", vbuf.at[pl.ds(0, nx - 1)], rs.at[VAL]).wait_recv()
    for off in far + near:
        forward(2 * chip(off) + core).start()
    for k in range(nb):
        span = slice(k * BLOCK, (k + 1) * BLOCK)
        gin_acc[span, :first] = tn_dot(grad_t[k], first_at[k])
        gin_acc[span, first:] = tn_dot(grad_t[k], second_at[k])
    all_of("t", vbuf.at[pl.ds(0, nx)], rs.at[FWD]).wait_recv()
    tiles = 4
    width = feats // tiles
    for i in range(tiles):
        cols = slice(i * width, (i + 1) * width)
        acc = gin_acc[:, cols]
        for j in range(nt):
            acc = acc + nt_dot(vbuf[j], wbuf[j, cols, :])
        gin_v[:, cols] = acc.astype(BF16)
    gin_out = pltpu.make_async_copy(gin_v, gin_hbm, loc.at[0])
    gin_out.start()

    arrived(CNT, "y", all_ten)
    local[7].wait()
    hits = jnp.where(all_ten[:, :, 0, :] == d, 1.0, 0.0).astype(F32)
    count = jnp.sum(hits) * BLOCK
    quota = jnp.full((8, 128), quo_s[d], jnp.int32).astype(F32)
    scale = (quota / jnp.maximum(jnp.full((8, 128), count, F32), 1.0))[:1, :1]
    arrived(HY, "y", hz1)
    acc = hz1[0].astype(F32)
    for j in range(1, ny):
        acc = acc + hz1[j].astype(F32)
    da_v[:, :first] = acc[:, :first] * scale
    db_v[...] = acc[:, first:] * scale
    up_out = pltpu.make_async_copy(db_v, db_hbm, loc.at[2])
    up_out.start()
    arrived(HZ, "z", hz2)
    acc = hz2[0].astype(F32)
    for j in range(1, nz):
        acc = acc + hz2[j].astype(F32)
    da_v[:, first:] = acc * scale
    down_out = pltpu.make_async_copy(da_v, da_hbm, loc.at[3])
    down_out.start()

    base = both(x)
    if far + near:
        all_of("t", ebuf.at[pl.ds(0, nx - 1)], rs.at[BASE]).wait_recv()
    for off in far + near:
        base = base + ebuf[chip(off)].astype(F32)
    for k in range(nb):
        span = slice(k * BLOCK, (k + 1) * BLOCK)
        raised = tn_dot(low_t[k], up_at[k])
        out_v[span, :] = (base[span] + ADAPTER_SCALE * raised).astype(BF16)

    value_out = pltpu.make_async_copy(out_v, out_hbm, loc.at[1])
    value_out.start()

    left(TZ, "z", tz_v)
    left(TY, "y", ty_v)
    left(AZ, "z", row1)
    left(AY, "y", col2)
    left(CNT, "y", all_ten)
    for k in range(1, nb):
        left(SY2, "y", s1.at[k])
        left(SZ2, "z", s2.at[k])
    left_both(RANK, "t", pbuf)
    left_both(GZ, "z", gz_v)
    left_both(GY, "y", gy_v)
    left(WGT, "t", wbuf, 1 + len(near_weights[1::2]))
    for kind in (WGT, SHARE):
        if count_shared:
            all_of("t", wbuf.at[pl.ds(0, count_shared), pl.ds(0, rows_half)], rs.at[0], kind).wait_send()
    left(VAL, "t", vbuf, nx - 1)
    left(FWD, "t", vbuf, nx)
    left(PRE, "t", presend, nx)
    left(BASE, "t", bsend, nx - 1)
    left(HY, "y", h1)
    left(HZ, "z", h2)
    for copy in (gin_out, value_out, up_out, down_out):
        copy.wait()


def write_out(out_v, gin_v, da_v, db_v, out_hbm, gin_hbm, da_hbm, db_hbm, sems):
    pairs = ((gin_v, gin_hbm), (out_v, out_hbm), (da_v, da_hbm), (db_v, db_hbm))
    copies = [pltpu.make_async_copy(a, b, sems.at[i]) for i, (a, b) in enumerate(pairs)]
    for copy in copies:
        copy.start()
    for copy in copies:
        copy.wait()


def solution(mesh):
    nt = mesh.shape["tensor"]
    nz = LINE
    ny = mesh.shape["dp"] // nz

    def on_device(x, w, a, b, v, tenants, quotas):
        rows, feats = x.shape
        values = v.shape[1]
        _, rank, _ = b.shape
        nb = tenants.shape[0]
        first = feats // 2
        wide, half = first + values, feats - first
        hbm = pl.BlockSpec(memory_space=pltpu.MemorySpace.HBM)
        anywhere = pl.BlockSpec(memory_space=pl.ANY)
        out, gin, da, db = pl.pallas_call(
            functools.partial(kernel, nt, ny, nz),
            out_shape=(
                jax.ShapeDtypeStruct((rows, values), BF16),
                jax.ShapeDtypeStruct((rows, feats), BF16),
                jax.ShapeDtypeStruct((rank, feats), F32),
                jax.ShapeDtypeStruct((rank, values), F32),
            ),
            in_specs=[hbm] * 7,
            out_specs=(anywhere,) * 4,
            scratch_shapes=[
                pltpu.VMEM((rows, values), BF16),
                pltpu.VMEM((rows, feats), BF16),
                pltpu.VMEM((rank, feats), F32),
                pltpu.VMEM((rank, values), F32),
                pltpu.SMEM((nb,), jnp.int32),
                pltpu.SMEM(quotas.shape, jnp.int32),
                pltpu.VMEM((1, 128), jnp.int32),
                pltpu.VMEM((nz, 1, 128), jnp.int32),
                pltpu.VMEM((ny, 1, 128), jnp.int32),
                pltpu.SMEM((nz, 1, 128), jnp.int32),
                pltpu.SMEM((ny, 1, 128), jnp.int32),
                pltpu.VMEM((ny, nz, 1, 128), jnp.int32),
                pltpu.VMEM((rows, feats), BF16),
                pltpu.VMEM((nz, rank, wide), BF16),
                pltpu.VMEM((ny, rank, half), BF16),
                pltpu.VMEM((nb, ny, rank, wide), BF16),
                pltpu.VMEM((nb, nz, rank, half), BF16),
                pltpu.VMEM((ny, rank, wide), BF16),
                pltpu.VMEM((ny, rank, wide), BF16),
                pltpu.VMEM((nz, rank, half), BF16),
                pltpu.VMEM((nz, rank, half), BF16),
                pltpu.VMEM((nt, rows, values), BF16),
                pltpu.VMEM((nt, feats, values), BF16),
                pltpu.VMEM((nb, nt, 2 * rank, BLOCK), BF16),
                pltpu.VMEM((nt // 2, rows, values), BF16),
                pltpu.VMEM((nt // 2, rows, values), BF16),
                pltpu.VMEM((nt // 2, rows, values), F32),
                pltpu.VMEM((nt // 2, rows, values), BF16),
                pltpu.VMEM((nt // 2, rows, values), BF16),
                pltpu.VMEM((nb, rank, wide), BF16),
                pltpu.VMEM((nb, rank, half), BF16),
                pltpu.VMEM((nb, nz, rank, wide), BF16),
                pltpu.VMEM((nb, ny, rank, half), BF16),
                pltpu.VMEM((ny, rank, wide), F32),
                pltpu.VMEM((nz, rank, half), F32),
                pltpu.VMEM((ny, rank, wide), BF16),
                pltpu.VMEM((nz, rank, half), BF16),
                pltpu.VMEM((ny, rank, wide), BF16),
                pltpu.VMEM((nz, rank, half), BF16),
                pltpu.VMEM((rows, feats), F32),
                pltpu.SemaphoreType.DMA((8,)),
                pltpu.SemaphoreType.DMA((SZ2 + 1,)),
                pltpu.SemaphoreType.DMA((KINDS,)),
                pltpu.SemaphoreType.DMA((nt,)),
                pltpu.SemaphoreType.DMA((nt // 2,)),
            ],
            compiler_params=pltpu.CompilerParams(
                collective_id=0, has_side_effects=True, vmem_limit_bytes=48 << 20
            ),
        )(*[
            pltpu.with_memory_space_constraint(arg, pltpu.MemorySpace.HBM)
            for arg in (tenants, quotas, x, w, jnp.swapaxes(a[0], 0, 1), b[0], v)
        ])
        out, gin, da, db = pl.pallas_call(
            write_out,
            out_shape=(
                jax.ShapeDtypeStruct((rows, values), BF16),
                jax.ShapeDtypeStruct((rows, feats), BF16),
                jax.ShapeDtypeStruct((rank, feats), F32),
                jax.ShapeDtypeStruct((rank, values), F32),
            ),
            in_specs=[anywhere] * 4,
            out_specs=(hbm,) * 4,
            scratch_shapes=[pltpu.SemaphoreType.DMA((4,))],
            compiler_params=pltpu.CompilerParams(vmem_limit_bytes=4 << 20),
        )(out, gin, da, db)
        return out, gin, jnp.swapaxes(da, 0, 1)[None], db[None]

    return jax.shard_map(
        on_device,
        mesh=mesh,
        in_specs=(
            P("dp", "tensor"),
            P(None, "tensor"),
            P("dp", "tensor", None),
            P("dp", None, "tensor"),
            P("dp", "tensor"),
            P("dp"),
            P(),
        ),
        out_specs=(
            P("dp", "tensor"),
            P("dp", "tensor"),
            P("dp", "tensor", None),
            P("dp", None, "tensor"),
        ),
        check_vma=False,
    )
```

```python
import functools

import jax
import jax.numpy as jnp
from jax import lax
from jax.experimental import pallas as pl
from jax.experimental.pallas import tpu as pltpu
from jax.sharding import PartitionSpec as P

MESH = pl.DeviceIdType.MESH
BLOCK = 128
LINE = 8
ADAPTER_SCALE = 2.0
BF16 = jnp.bfloat16
F32 = jnp.float32

TZ, TY, AZ, AY, VAL, FWD, BASE, HY, HZ, CNT, SY, SZ, RANK, GZ, GY, WGT, PRE, SHARE, SY2, SZ2, GZ2, GY2 = range(22)
SECOND = 12
KINDS = SECOND + GY + 1


def far_first(n):
    return sorted(range(1, n), key=lambda off: (-min(off, n - off), off))


def nt_dot(a, b):
    return lax.dot_general(a, b, (((1,), (1,)), ((), ())), preferred_element_type=F32)


def tn_dot(a, b):
    return lax.dot_general(a, b, (((0,), (0,)), ((), ())), preferred_element_type=F32)


def kernel(
    nt, ny, nz,
    ten_hbm, quo_hbm, x_hbm, w_hbm, a_hbm, b_hbm, v_hbm,
    out_hbm, gin_hbm, da_hbm, db_hbm,
    out_v, gin_v, da_v, db_v, ten_s, quo_s, tile, tz_v, ty_v, tz_s, ty_s, all_ten,
    xv, row1, col2, s1, s2, r1_first, r1_second, r2_first, r2_second,
    vbuf, wbuf, pbuf, presend, prebuf, keep, bsend, ebuf, g1, g2, gz_v, gy_v, acc1, acc2, h1, h2, hz1, hz2, gin_acc,
    loc, ss, rs, wgt_rs, pre_rs,
):
    t = lax.axis_index("tensor")
    d = lax.axis_index("dp")
    y, z = lax.div(d, nz), lax.rem(d, nz)
    nx = nt // 2
    x, core = lax.div(t, 2), lax.rem(t, 2)
    twin = t + 1 - 2 * core
    rows, feats = xv.shape
    nb = rows // BLOCK
    rank, half = col2.shape[1:]
    r1, r2 = (r1_first, r1_second), (r2_first, r2_second)
    first = feats - half
    values = v_hbm.shape[1]
    wide = first + values
    cut1, cut2 = pl.cdiv(wide, 256) * 128, half // 2
    parts1, parts2 = (pl.ds(0, cut1), pl.ds(cut1, wide - cut1)), (pl.ds(0, cut2), pl.ds(cut2, half - cut2))

    lines = {
        "t": (t, nt, lambda p: {"tensor": p}),
        "y": (y, ny, lambda p: {"dp": p * nz + z}),
        "z": (z, nz, lambda p: {"dp": y * nz + p}),
    }

    def remote(kind, line, src, dst, peer, recv=None):
        return pltpu.make_async_remote_copy(
            src_ref=src, dst_ref=dst, send_sem=ss.at[kind], recv_sem=rs.at[kind] if recv is None else recv,
            device_id=lines[line][2](peer), device_id_type=MESH,
        )

    def all_of(line, buf, recv, send=0):
        me, n, dev = lines[line]
        return pltpu.make_async_remote_copy(
            src_ref=buf, dst_ref=buf, send_sem=ss.at[send], recv_sem=recv,
            device_id=dev(lax.rem(me + 1, n)), device_id_type=MESH,
        )

    def arrived(kind, line, buf):
        others = lines[line][1] - 1
        if others:
            all_of(line, buf.at[pl.ds(0, others)], rs.at[kind]).wait_recv()

    def part_arrived(kind, line, buf, part):
        others = lines[line][1] - 1
        if others:
            all_of(line, buf.at[pl.ds(0, others), :, part], rs.at[kind]).wait_recv()

    def left(kind, line, buf, copies=None):
        others = lines[line][1] - 1 if copies is None else copies
        if others:
            all_of(line, buf.at[pl.ds(0, others)], rs.at[0], kind).wait_send()

    def left_both(kind, line, buf):
        others = lines[line][1] - 1
        if others:
            all_of(line, buf.at[:, pl.ds(0, others)], rs.at[0], kind).wait_send()

    def peers(line, fn):
        me, n, _ = lines[line]
        for off in far_first(n):
            fn(lax.rem(me + off, n))

    def each(line, fn):
        me, n, _ = lines[line]

        def body(off, carry):
            fn(lax.rem(me + off, n))
            return carry

        lax.fori_loop(1, n, body, 0)

    barrier = pltpu.get_barrier_semaphore()
    for line in ("t", "y", "z"):
        dev = lines[line][2]
        each(line, lambda p: pl.semaphore_signal(barrier, inc=1, device_id=dev(p), device_id_type=MESH))
    local = [
        pltpu.make_async_copy(ten_hbm, ten_s, loc.at[0]),
        pltpu.make_async_copy(a_hbm.at[:, pl.ds(0, first)], row1.at[z, :, pl.ds(0, first)], loc.at[1]),
        pltpu.make_async_copy(b_hbm, row1.at[z, :, pl.ds(first, values)], loc.at[2]),
        pltpu.make_async_copy(a_hbm.at[:, pl.ds(first, half)], col2.at[y], loc.at[3]),
        pltpu.make_async_copy(x_hbm, xv, loc.at[4]),
        pltpu.make_async_copy(v_hbm, vbuf.at[t], loc.at[5]),
        pltpu.make_async_copy(w_hbm.at[pl.ds(t * feats, feats)], wbuf.at[t], loc.at[6]),
        pltpu.make_async_copy(quo_hbm, quo_s, loc.at[7]),
    ]
    for copy in local:
        copy.start()
    local[0].wait()
    lane = lax.broadcasted_iota(jnp.int32, tile.shape, 1)
    mine = jnp.full(tile.shape, -1, jnp.int32)
    for k in range(nb):
        mine = jnp.where(lane == k, ten_s[k], mine)
    tile[...] = mine
    tz_v[z] = mine
    ty_v[y] = mine
    for copy in local[1:4]:
        copy.wait()
    pl.semaphore_wait(barrier, nt + ny + nz - 3)

    peers("z", lambda p: remote(TZ, "z", tile, tz_v.at[z], p).start())
    peers("y", lambda p: remote(TY, "y", tile, ty_v.at[y], p).start())
    peers("z", lambda p: remote(AZ, "z", row1.at[z], row1.at[z], p).start())
    peers("y", lambda p: remote(AY, "y", col2.at[y], col2.at[y], p).start())

    near = [off for off in range(1, nx) if min(off, nx - off) == 1]
    far = [off for off in range(1, nx) if off not in near]

    def chip(off):
        return lax.rem(x + off, nx)

    def value_to(p):
        return remote(VAL, "t", vbuf.at[t], vbuf.at[t], p)

    def weight_to(p, part=0, parts=1):
        size = feats // parts
        return remote(
            WGT, "t", w_hbm.at[pl.ds(p * feats + part * size, size)],
            wbuf.at[t, pl.ds(part * size, size)], p, wgt_rs.at[t],
        )

    def weight_arrived(p):
        all_of("t", wbuf.at[p], wgt_rs.at[p]).wait_recv()

    def pair(offs):
        return [2 * chip(off) + c for off in offs for c in (core, 1 - core)]

    ways = [(line, step) for line in ("y", "z") for step in (1, -1) if lines[line][1] > 1]
    mine_half = lax.rem(y + z, 2)
    rows_half = feats // 2
    rows_share = rows_half // len(ways)

    def share(p, i):
        line, step = ways[i]
        me, n, _ = lines[line]
        span = pl.ds(mine_half * rows_half + i * rows_share, rows_share)
        return remote(SHARE, line, wbuf.at[p, span], wbuf.at[p, span], lax.rem(me + step + n, n))

    near_weights = pair(near)
    shared = (pair(far), near_weights[::2])
    count_shared = len(shared[0]) + len(shared[1])
    weight_to(twin).start()
    for p in shared[0] + shared[1]:
        weight_to(p, mine_half, 2).start()
    for p in near_weights[1::2]:
        weight_to(p, 0, 4).start()

    arrived(TZ, "z", tz_v)
    arrived(TY, "y", ty_v)
    to_z = pltpu.make_async_copy(tz_v, tz_s, loc.at[0])
    to_y = pltpu.make_async_copy(ty_v, ty_s, loc.at[1])
    to_z.start()
    to_y.start()
    all_ten[y] = tz_v[...]
    to_z.wait()
    to_y.wait()

    def pick1(k, p):
        return row1[lax.rem(ty_s[p, 0, k], nz)]

    def pick2(k, p):
        return col2[lax.div(tz_s[p, 0, k], nz)]

    def send1(k, p):
        s1[k, p] = pick1(k, p)
        kind, recv = (SY if k == 0 else SY2), rs.at[SY + k * SECOND]
        remote(kind, "y", s1.at[k, p], r1[k].at[y], p, recv).start()

    def send2(k, p):
        s2[k, p] = pick2(k, p)
        kind, recv = (SZ if k == 0 else SZ2), rs.at[SZ + k * SECOND]
        remote(kind, "z", s2.at[k, p], r2[k].at[z], p, recv).start()

    arrived(AZ, "z", row1)
    peers("y", lambda p: send1(0, p))
    arrived(AY, "y", col2)
    peers("z", lambda p: send2(0, p))
    for k in range(nb):
        r1[k][y] = pick1(k, y)
        r2[k][z] = pick2(k, z)

    def base_of(p):
        return jnp.dot(xv[...], wbuf[p], preferred_element_type=F32)

    def pre_to(q):
        return pltpu.make_async_remote_copy(
            src_ref=presend.at[q], dst_ref=prebuf.at[q], send_sem=ss.at[PRE], recv_sem=pre_rs.at[q],
            device_id={"tensor": twin}, device_id_type=MESH,
        )

    def halves(q):
        presend[q] = base_of(2 * q + 1 - core).astype(BF16)
        pre_to(q).start()
        keep[q] = base_of(2 * q + core)

    def both(q):
        pre_to(q).wait_recv()
        return keep[q] + prebuf[q].astype(F32)

    def base_to(q):
        return pltpu.make_async_remote_copy(
            src_ref=bsend.at[q], dst_ref=ebuf.at[x], send_sem=ss.at[BASE], recv_sem=rs.at[BASE],
            device_id={"tensor": 2 * q + core}, device_id_type=MESH,
        )

    def send_base(q):
        bsend[q] = both(q).astype(BF16)
        base_to(q).start()

    def forward(p):
        return pltpu.make_async_remote_copy(
            src_ref=vbuf.at[p], dst_ref=vbuf.at[p], send_sem=ss.at[FWD], recv_sem=rs.at[FWD],
            device_id={"tensor": twin}, device_id_type=MESH,
        )

    local[4].wait()
    local[5].wait()
    local[6].wait()
    weight_arrived(twin)
    halves(x)
    left(SY, "y", s1.at[0])
    left(SZ, "z", s2.at[0])

    def send_rest():
        for k in range(1, nb):
            peers("y", lambda p: send1(k, p))
            peers("z", lambda p: send2(k, p))

    pl.when(core == 0)(send_rest)
    for group in shared:
        for p in group:
            all_of("t", wbuf.at[p, pl.ds(0, rows_half)], wgt_rs.at[p]).wait_recv()
        if group is shared[0]:
            pl.when(core == 1)(send_rest)
        for i in range(len(ways)):
            for p in group:
                share(p, i).start()
    peers("y", lambda p: remote(CNT, "y", tz_v, all_ten.at[y], p).start())

    first_at, second_at, up_at = [], [], []

    def rank_products(k):
        arrived(SY + k * SECOND, "y", r1[k])
        arrived(SZ + k * SECOND, "z", r2[k])
        tenant = ten_s[k]
        part1 = r1[k][lax.div(tenant, nz)]
        at2 = r2[k][lax.rem(tenant, nz)]
        at1, up = part1[:, :first], part1[:, first:]
        first_at.append(at1)
        second_at.append(at2)
        up_at.append(up)
        span = pl.ds(k * BLOCK, BLOCK)
        low = nt_dot(at1, xv[span, :first]) + nt_dot(at2, xv[span, first:])
        grad = ADAPTER_SCALE * nt_dot(up, vbuf[t, span, :])
        pbuf[k, t, :rank] = low.astype(BF16)
        pbuf[k, t, rank:] = grad.astype(BF16)
        recv = rs.at[RANK + k * SECOND]
        peers("t", lambda p: remote(RANK, "t", pbuf.at[k, t], pbuf.at[k, t], p, recv).start())

    low_t, grad_t = [], []

    def block_gradients(k):
        arrived(RANK + k * SECOND, "t", pbuf.at[k])
        total = pbuf[k, 0].astype(F32)
        for j in range(1, nt):
            total = total + pbuf[k, j].astype(F32)
        low_k, grad_k = total[:rank].astype(BF16), total[rank:].astype(BF16)
        low_t.append(low_k)
        grad_t.append(grad_k)
        span = slice(k * BLOCK, (k + 1) * BLOCK)
        g1[k, :, :first] = jnp.dot(grad_k, xv[span, :first], preferred_element_type=F32).astype(BF16)
        g1[k, :, first:] = (
            ADAPTER_SCALE * jnp.dot(low_k, vbuf[t, span, :], preferred_element_type=F32)
        ).astype(BF16)
        g2[k] = jnp.dot(grad_k, xv[span, first:], preferred_element_type=F32).astype(BF16)
        kinds_z, kinds_y = (GZ + k * SECOND, GZ2), (GY + k * SECOND, GY2)
        whole = k < nb - 1
        for at1, at2, kz, ky in zip(
            (pl.ds(0, wide),) if whole else parts1, (pl.ds(0, half),) if whole else parts2, kinds_z, kinds_y
        ):
            recv_z, recv_y = rs.at[kz], rs.at[ky]
            peers("z", lambda p: remote(GZ, "z", g1.at[k, :, at1], gz_v.at[k, z, :, at1], p, recv_z).start())
            peers("y", lambda p: remote(GY, "y", g2.at[k, :, at2], gy_v.at[k, y, :, at2], p, recv_y).start())
        gz_v[k, z] = g1[k]
        gy_v[k, y] = g2[k]

    rank_products(0)
    for p in near_weights[1::2]:
        weight_to(p, 1, 4).start()
    rank_products(1)
    for part in range(2, 4):
        for p in near_weights[1::2]:
            weight_to(p, part, 4).start()
    for off in far + near:
        value_to(2 * chip(off) + core).start()
    forward(t).start()
    block_gradients(0)
    block_gradients(1)

    if count_shared:
        all_of("t", wbuf.at[pl.ds(0, count_shared), pl.ds(0, rows_half)], rs.at[SHARE]).wait_recv()
    for off in far:
        halves(chip(off))
    for off in far:
        send_base(chip(off))

    def add_up(k, p, owner, ten, buf, acc, part):
        total = acc[p, :, part]
        for j in range(buf.shape[1]):
            hit = jnp.where(ten[j, 0, k] == owner, 1.0, 0.0).astype(F32)
            total = total + hit * buf[k, j, :, part].astype(F32)
        return total

    def add1(k, p, part=slice(None)):
        return add_up(k, p, p * nz + z, tz_s, gz_v, acc1, part)

    def add2(k, p, part=slice(None)):
        return add_up(k, p, y * nz + p, ty_s, gy_v, acc2, part)

    acc1[...] = jnp.zeros_like(acc1)
    acc2[...] = jnp.zeros_like(acc2)
    for k in range(nb - 1):
        arrived(GZ + k * SECOND, "z", gz_v.at[k])
        arrived(GY + k * SECOND, "y", gy_v.at[k])

        def keep1(p, carry):
            acc1[p] = add1(k, p)
            return carry

        def keep2(p, carry):
            acc2[p] = add2(k, p)
            return carry

        lax.fori_loop(0, ny, keep1, 0)
        lax.fori_loop(0, nz, keep2, 0)

    for p in near_weights[1::2]:
        weight_arrived(p)
    for off in near:
        halves(chip(off))
    last = nb - 1

    def send_sum1(p, part):
        h1[p, :, part] = add1(last, p, part).astype(BF16)
        remote(HY, "y", h1.at[p, :, part], hz1.at[y, :, part], p).start()

    def send_sum2(p, part):
        h2[p, :, part] = add2(last, p, part).astype(BF16)
        remote(HZ, "z", h2.at[p, :, part], hz2.at[z, :, part], p).start()

    for at1, at2, kz, ky in zip(parts1, parts2, (GZ + last * SECOND, GZ2), (GY + last * SECOND, GY2)):
        part_arrived(kz, "z", gz_v.at[last], at1)
        peers("y", lambda p: send_sum1(p, at1))
        part_arrived(ky, "y", gy_v.at[last], at2)
        peers("z", lambda p: send_sum2(p, at2))
    hz1[y] = add1(last, y).astype(BF16)
    hz2[z] = add2(last, z).astype(BF16)
    for off in near:
        send_base(chip(off))

    if far + near:
        all_of("t", vbuf.at[pl.ds(0, nx - 1)], rs.at[VAL]).wait_recv()
    for off in far + near:
        forward(2 * chip(off) + core).start()
    for k in range(nb):
        span = slice(k * BLOCK, (k + 1) * BLOCK)
        gin_acc[span, :first] = tn_dot(grad_t[k], first_at[k])
        gin_acc[span, first:] = tn_dot(grad_t[k], second_at[k])
    all_of("t", vbuf.at[pl.ds(0, nx)], rs.at[FWD]).wait_recv()
    tiles = 4
    width = feats // tiles
    for i in range(tiles):
        cols = slice(i * width, (i + 1) * width)
        acc = gin_acc[:, cols]
        for j in range(nt):
            acc = acc + nt_dot(vbuf[j], wbuf[j, cols, :])
        gin_v[:, cols] = acc.astype(BF16)
    gin_out = pltpu.make_async_copy(gin_v, gin_hbm, loc.at[0])
    gin_out.start()

    arrived(CNT, "y", all_ten)
    local[7].wait()
    hits = jnp.where(all_ten[:, :, 0, :] == d, 1.0, 0.0).astype(F32)
    count = jnp.sum(hits) * BLOCK
    quota = jnp.full((8, 128), quo_s[d], jnp.int32).astype(F32)
    scale = (quota / jnp.maximum(jnp.full((8, 128), count, F32), 1.0))[:1, :1]
    arrived(HY, "y", hz1)
    acc = hz1[0].astype(F32)
    for j in range(1, ny):
        acc = acc + hz1[j].astype(F32)
    da_v[:, :first] = acc[:, :first] * scale
    db_v[...] = acc[:, first:] * scale
    up_out = pltpu.make_async_copy(db_v, db_hbm, loc.at[2])
    up_out.start()
    arrived(HZ, "z", hz2)
    acc = hz2[0].astype(F32)
    for j in range(1, nz):
        acc = acc + hz2[j].astype(F32)
    da_v[:, first:] = acc * scale
    down_out = pltpu.make_async_copy(da_v, da_hbm, loc.at[3])
    down_out.start()

    base = both(x)
    if far + near:
        all_of("t", ebuf.at[pl.ds(0, nx - 1)], rs.at[BASE]).wait_recv()
    for off in far + near:
        base = base + ebuf[chip(off)].astype(F32)
    for k in range(nb):
        span = slice(k * BLOCK, (k + 1) * BLOCK)
        raised = tn_dot(low_t[k], up_at[k])
        out_v[span, :] = (base[span] + ADAPTER_SCALE * raised).astype(BF16)

    value_out = pltpu.make_async_copy(out_v, out_hbm, loc.at[1])
    value_out.start()

    left(TZ, "z", tz_v)
    left(TY, "y", ty_v)
    left(AZ, "z", row1)
    left(AY, "y", col2)
    left(CNT, "y", all_ten)
    for k in range(1, nb):
        left(SY2, "y", s1.at[k])
        left(SZ2, "z", s2.at[k])
    left_both(RANK, "t", pbuf)
    left_both(GZ, "z", gz_v)
    left_both(GY, "y", gy_v)
    left(WGT, "t", wbuf, 1 + len(near_weights[1::2]))
    for kind in (WGT, SHARE):
        if count_shared:
            all_of("t", wbuf.at[pl.ds(0, count_shared), pl.ds(0, rows_half)], rs.at[0], kind).wait_send()
    left(VAL, "t", vbuf, nx - 1)
    left(FWD, "t", vbuf, nx)
    left(PRE, "t", presend, nx)
    left(BASE, "t", bsend, nx - 1)
    left(HY, "y", h1)
    left(HZ, "z", h2)
    for copy in (gin_out, value_out, up_out, down_out):
        copy.wait()


def write_out(out_v, gin_v, da_v, db_v, out_hbm, gin_hbm, da_hbm, db_hbm, sems):
    pairs = ((gin_v, gin_hbm), (out_v, out_hbm), (da_v, da_hbm), (db_v, db_hbm))
    copies = [pltpu.make_async_copy(a, b, sems.at[i]) for i, (a, b) in enumerate(pairs)]
    for copy in copies:
        copy.start()
    for copy in copies:
        copy.wait()


def solution(mesh):
    nt = mesh.shape["tensor"]
    nz = LINE
    ny = mesh.shape["dp"] // nz

    def on_device(x, w, a, b, v, tenants, quotas):
        rows, feats = x.shape
        values = v.shape[1]
        _, rank, _ = b.shape
        nb = tenants.shape[0]
        first = feats // 2
        wide, half = first + values, feats - first
        hbm = pl.BlockSpec(memory_space=pltpu.MemorySpace.HBM)
        anywhere = pl.BlockSpec(memory_space=pl.ANY)
        out, gin, da, db = pl.pallas_call(
            functools.partial(kernel, nt, ny, nz),
            out_shape=(
                jax.ShapeDtypeStruct((rows, values), BF16),
                jax.ShapeDtypeStruct((rows, feats), BF16),
                jax.ShapeDtypeStruct((rank, feats), F32),
                jax.ShapeDtypeStruct((rank, values), F32),
            ),
            in_specs=[hbm] * 7,
            out_specs=(anywhere,) * 4,
            scratch_shapes=[
                pltpu.VMEM((rows, values), BF16),
                pltpu.VMEM((rows, feats), BF16),
                pltpu.VMEM((rank, feats), F32),
                pltpu.VMEM((rank, values), F32),
                pltpu.SMEM((nb,), jnp.int32),
                pltpu.SMEM(quotas.shape, jnp.int32),
                pltpu.VMEM((1, 128), jnp.int32),
                pltpu.VMEM((nz, 1, 128), jnp.int32),
                pltpu.VMEM((ny, 1, 128), jnp.int32),
                pltpu.SMEM((nz, 1, 128), jnp.int32),
                pltpu.SMEM((ny, 1, 128), jnp.int32),
                pltpu.VMEM((ny, nz, 1, 128), jnp.int32),
                pltpu.VMEM((rows, feats), BF16),
                pltpu.VMEM((nz, rank, wide), BF16),
                pltpu.VMEM((ny, rank, half), BF16),
                pltpu.VMEM((nb, ny, rank, wide), BF16),
                pltpu.VMEM((nb, nz, rank, half), BF16),
                pltpu.VMEM((ny, rank, wide), BF16),
                pltpu.VMEM((ny, rank, wide), BF16),
                pltpu.VMEM((nz, rank, half), BF16),
                pltpu.VMEM((nz, rank, half), BF16),
                pltpu.VMEM((nt, rows, values), BF16),
                pltpu.VMEM((nt, feats, values), BF16),
                pltpu.VMEM((nb, nt, 2 * rank, BLOCK), BF16),
                pltpu.VMEM((nt // 2, rows, values), BF16),
                pltpu.VMEM((nt // 2, rows, values), BF16),
                pltpu.VMEM((nt // 2, rows, values), F32),
                pltpu.VMEM((nt // 2, rows, values), BF16),
                pltpu.VMEM((nt // 2, rows, values), BF16),
                pltpu.VMEM((nb, rank, wide), BF16),
                pltpu.VMEM((nb, rank, half), BF16),
                pltpu.VMEM((nb, nz, rank, wide), BF16),
                pltpu.VMEM((nb, ny, rank, half), BF16),
                pltpu.VMEM((ny, rank, wide), F32),
                pltpu.VMEM((nz, rank, half), F32),
                pltpu.VMEM((ny, rank, wide), BF16),
                pltpu.VMEM((nz, rank, half), BF16),
                pltpu.VMEM((ny, rank, wide), BF16),
                pltpu.VMEM((nz, rank, half), BF16),
                pltpu.VMEM((rows, feats), F32),
                pltpu.SemaphoreType.DMA((8,)),
                pltpu.SemaphoreType.DMA((SZ2 + 1,)),
                pltpu.SemaphoreType.DMA((KINDS,)),
                pltpu.SemaphoreType.DMA((nt,)),
                pltpu.SemaphoreType.DMA((nt // 2,)),
            ],
            compiler_params=pltpu.CompilerParams(
                collective_id=0, has_side_effects=True, vmem_limit_bytes=48 << 20
            ),
        )(*[
            pltpu.with_memory_space_constraint(arg, pltpu.MemorySpace.HBM)
            for arg in (tenants, quotas, x, w, jnp.swapaxes(a[0], 0, 1), b[0], v)
        ])
        out, gin, da, db = pl.pallas_call(
            write_out,
            out_shape=(
                jax.ShapeDtypeStruct((rows, values), BF16),
                jax.ShapeDtypeStruct((rows, feats), BF16),
                jax.ShapeDtypeStruct((rank, feats), F32),
                jax.ShapeDtypeStruct((rank, values), F32),
            ),
            in_specs=[anywhere] * 4,
            out_specs=(hbm,) * 4,
            scratch_shapes=[pltpu.SemaphoreType.DMA((4,))],
            compiler_params=pltpu.CompilerParams(vmem_limit_bytes=4 << 20),
        )(out, gin, da, db)
        return out, gin, jnp.swapaxes(da, 0, 1)[None], db[None]

    return jax.shard_map(
        on_device,
        mesh=mesh,
        in_specs=(
            P("dp", "tensor"),
            P(None, "tensor"),
            P("dp", "tensor", None),
            P("dp", None, "tensor"),
            P("dp", "tensor"),
            P("dp"),
            P(),
        ),
        out_specs=(
            P("dp", "tensor"),
            P("dp", "tensor"),
            P("dp", "tensor", None),
            P("dp", None, "tensor"),
        ),
        check_vma=False,
    )
```
